32 devices in a mesh: groups: 2 (over y), frames: 4 (over z), heads: 4 (over x, core).
Axes of the slice: x: 2, y: 2, z: 4, core: 2. Of those that a mesh axis runs over, the one named last changes fastest.
Arguments:
- tokens: bfloat16 [64, 128, 1024], P(('groups', 'frames')), parts along dimension 0, may hold values from -12 to 12
- w_qkv: bfloat16 [1024, 3, 1024], P(None, None, 'heads'), may hold values from -1 to 1
- w_out: bfloat16 [1024, 1024], P('heads'), may hold values from -2 to 2
- pair_slots: int32 [16, 2], P(('groups', 'frames')), parts along dimension 0, may hold values from -1 to 31, as said below
Outputs:
- mixed: bfloat16 [64, 128, 1024], P(('groups', 'frames'), 'heads'), parts along dimension 0
The draws below stay inside these ranges and needn't reach their ends.
There are 2 independent parts, one for each index of `groups`. The reference program is written for one: setup_inputs(seed, part) draws one part's arguments, and reference() takes and returns one part's arrays. A program takes and returns all parts, laid end to end along the dimension named above; an argument that names none is the same for every part. Nothing has to cross between parts.
Inputs may be any that keep to these rules, and one draw needn't show every extreme that they name: `pair_slots`: rows 2 * o to 2 * o + 1 are the pairs owned by device o of the frames axis, which holds frames 8 * o to 8 * o + 7. A row is two frame indices or -1 twice; in each owner's block the live rows come first, and one owner has all 2 rows live. In one owner's block no two entries of live rows belong to the same home device (frame index // 8), so a frame appears there at most once.
All inputs are finite; a program needn't handle non-finite values.
Results may differ from the reference program's by a relative error of at most 0.0081.
Values may be sent and summed in bfloat16 or wider, within the bound.
A program may use at most 64 MiB of HBM per device.

```python
import jax
import jax.numpy as jnp
from jax import lax

D = 1024
HD = 64
TOK_FR = 128
FR_DEV = 8
FRAMES = 32
CAP = 2
SLOTS = 8


def draw_tokens(key, part):
    base = jax.random.normal(jax.random.fold_in(key, 1), (FRAMES, TOK_FR, D), jnp.float32)
    return jnp.clip(base, -12.0, 12.0).astype(jnp.bfloat16)


def draw_w_qkv(key, part):
    scale = D ** (-0.5)
    query_part = jax.random.normal(jax.random.fold_in(key, 1), (D, D), jnp.float32) * (1.2 * scale)
    key_part = jax.random.normal(jax.random.fold_in(key, 2), (D, D), jnp.float32) * (1.2 * scale)
    value_part = jax.random.normal(jax.random.fold_in(key, 3), (D, D), jnp.float32) * scale
    stacked = jnp.stack([query_part, key_part, value_part], axis=1)
    return jnp.clip(stacked, -1.0, 1.0).astype(jnp.bfloat16)


def draw_pair_slots(key, part):
    owner_count = SLOTS // CAP

    def one_owner(owner):
        sub_key = jax.random.fold_in(key, owner)
        order = jax.random.permutation(jax.random.fold_in(sub_key, 1), owner_count)
        local = jax.random.randint(jax.random.fold_in(sub_key, 2), (2 * CAP,), 0, FR_DEV)
        chosen = order[:2 * CAP] * FR_DEV + local
        return chosen.reshape(CAP, 2)
    owners = jnp.arange(owner_count)
    listing = jax.vmap(one_owner)(owners)
    live_count = jax.random.randint(jax.random.fold_in(key, 3), (owner_count,), 1, CAP + 1)
    fullest = jax.random.randint(jax.random.fold_in(key, 4), (), 0, owner_count)
    live_count = jnp.where(owners == fullest, CAP, live_count)
    is_live = jnp.arange(CAP)[None, :] < live_count[:, None]
    listing = jnp.where(is_live[:, :, None], listing, -1)
    return listing.reshape(owner_count * CAP, 2).astype(jnp.int32)


def shard_levels(key, shape, cuts, least, high):
    level = 1.0
    for dim, parts in cuts:
        heights = jax.random.uniform(jax.random.fold_in(jax.random.fold_in(key, 6), dim), (parts,), jnp.float32, least / len(cuts), high / len(cuts))
        level = level * jnp.repeat(jnp.exp(heights), shape[dim] // parts).reshape((-1,) + (1,) * (len(shape) - 1 - dim))
    return level


def centred(own_key, shape, width, reach, split=(), dtype=jnp.bfloat16):
    array = jax.random.normal(own_key, shape, jnp.float32) * width
    if len(split) > 0:
        array = shard_levels(own_key, shape, split, -0.22, 0.18) * array
    return jnp.clip(array, min=-reach, max=reach).astype(dtype)


def setup_inputs(seed: int = 0, part: int = 0) -> dict:
    streams_of = jax.random.split(jax.random.key(seed), 5)
    own_keys = jax.random.split(jax.random.fold_in(streams_of[4], part), 5)
    tokens = draw_tokens(jax.random.fold_in(jax.random.fold_in(streams_of[4], part), 71), part)
    w_qkv = draw_w_qkv(jax.random.fold_in(streams_of[4], 71), part)
    w_out = centred(streams_of[2], (D, D), 8 ** -0.5, 2.0, ((0, 4),))
    pair_slots = draw_pair_slots(jax.random.fold_in(jax.random.fold_in(streams_of[4], part), 71), part)
    return dict(tokens=tokens, w_qkv=w_qkv, w_out=w_out, pair_slots=pair_slots)


def attend(queries, key_rows, values):
    length, breadth = queries.shape
    head_count = breadth // HD
    query_heads = queries.reshape(length, head_count, HD).astype(jnp.float32)
    key_heads = key_rows.reshape(key_rows.shape[0], head_count, HD).astype(jnp.float32)
    value_heads = values.reshape(values.shape[0], head_count, HD).astype(jnp.float32)
    scores = jnp.einsum("qhd,khd->hqk", query_heads, key_heads) * (HD ** -0.5)
    row_peak = jnp.max(scores, axis=2)
    lifted = jnp.exp(scores - row_peak[:, :, None])
    row_total = jnp.sum(lifted, axis=2)
    rounded = lifted.astype(jnp.bfloat16).astype(jnp.float32)
    weighted = jnp.einsum("hqk,khd->qhd", rounded, value_heads)
    normalized = weighted / jnp.transpose(row_total)[:, :, None]
    return normalized.reshape(length, breadth), row_peak + jnp.log(row_total)


def merge_into(state, frame, new_out, new_lse):
    acc_out, acc_lse = state
    old_out = acc_out[frame]
    old_lse = acc_lse[frame]
    ceiling = jnp.maximum(old_lse, new_lse)
    old_weight = jnp.exp(old_lse - ceiling)
    new_weight = jnp.exp(new_lse - ceiling)
    weight_total = old_weight + new_weight
    length, breadth = old_out.shape
    head_count = old_lse.shape[0]
    old_split = old_out.reshape(length, head_count, HD)
    new_split = new_out.reshape(length, head_count, HD)
    combined = (jnp.transpose(old_weight)[:, :, None] * old_split + jnp.transpose(new_weight)[:, :, None] * new_split) / jnp.transpose(weight_total)[:, :, None]
    acc_out = acc_out.at[frame].set(combined.reshape(length, breadth))
    acc_lse = acc_lse.at[frame].set(ceiling + jnp.log(weight_total))
    return acc_out, acc_lse


def reference(tokens, w_qkv, w_out, pair_slots):
    frames_all, length, width_model = tokens.shape
    packed = jnp.dot(tokens.reshape(frames_all * length, width_model), w_qkv.reshape(width_model, 3 * width_model), preferred_element_type=jnp.float32).astype(jnp.bfloat16)
    packed = packed.reshape(frames_all, length, 3 * width_model)
    queries = packed[:, :, :width_model]
    key_rows = packed[:, :, width_model:2 * width_model]
    values = packed[:, :, 2 * width_model:]

    def self_part(trio):
        return attend(trio[0], trio[1], trio[2])

    self_out, self_lse = lax.map(self_part, (queries, key_rows, values))

    def visit(state, slot_pair):
        first_frame = jnp.maximum(slot_pair[0], 0).astype(jnp.int32)
        second_frame = jnp.maximum(slot_pair[1], 0).astype(jnp.int32)

        def update(inner):
            out_first, lse_first = attend(queries[first_frame], key_rows[second_frame], values[second_frame])
            out_second, lse_second = attend(queries[second_frame], key_rows[first_frame], values[first_frame])
            inner = merge_into(inner, first_frame, out_first, lse_first)
            return merge_into(inner, second_frame, out_second, lse_second)

        def keep(inner):
            return inner

        return lax.cond(slot_pair[0] >= 0, update, keep, state), None

    final_state, _ = lax.scan(visit, (self_out, self_lse), pair_slots)
    merged = final_state[0].astype(jnp.bfloat16)
    mixed = jnp.dot(merged.reshape(frames_all * length, width_model), w_out, preferred_element_type=jnp.float32)
    return mixed.astype(jnp.bfloat16).reshape(frames_all, length, width_model)
```

```python
import functools

import jax
import jax.numpy as jnp
from jax import lax
from jax.experimental import pallas as pl
from jax.experimental.pallas import tpu as pltpu
from jax.sharding import PartitionSpec as P

HD = 64
MESH = pl.DeviceIdType.MESH


def repeat(count, body):
    if count <= 8:
        for step in range(count):
            body(step)
    else:

        def step_body(step, carry):
            body(step)
            return carry

        lax.fori_loop(0, count, step_body, 0)


def kernel(
    devices, parts, cap,
    pairs_ref, x_ref, w_ref, wo_ref, out_ref,
    listing, listing_s, q_ref, k_ref, v_ref, send1, recv1, send2, recv2,
    so, sm, sl, po, pm, psum, msend, mrecv, wall,
    list_send, list_recv, local_sem, h1_send, h1_recv, h2_send, h2_recv,
    w_send, w_recv, m_send, m_recv,
):
    me = lax.axis_index("frames")
    part = lax.axis_index("heads")
    frames_here, length, breadth = q_ref.shape
    width = x_ref.shape[1]
    heads = breadth // HD
    share = length // parts

    def frame_peer(step):
        return lax.rem(me + step, devices)

    def head_peer(step):
        return lax.rem(part + step, parts)

    barrier = pltpu.get_barrier_semaphore()

    def greet_frames(step):
        pl.semaphore_signal(
            barrier, inc=1, device_id={"frames": frame_peer(step + 1)}, device_id_type=MESH
        )

    def greet_heads(step):
        pl.semaphore_signal(
            barrier, inc=1, device_id={"heads": head_peer(step + 1)}, device_id_type=MESH
        )

    repeat(devices - 1, greet_frames)
    repeat(parts - 1, greet_heads)
    pl.semaphore_wait(barrier, devices + parts - 2)

    def list_copy(step):
        return pltpu.make_async_remote_copy(
            pairs_ref, listing.at[me], list_send.at[step], list_recv.at[step],
            device_id={"frames": frame_peer(step + 1)}, device_id_type=MESH,
        )

    def hop1(step):
        peer = frame_peer(step + 1)
        return pltpu.make_async_remote_copy(
            send1.at[peer], recv1.at[me], h1_send.at[step], h1_recv.at[step],
            device_id={"frames": peer}, device_id_type=MESH,
        )

    def hop2(step):
        peer = frame_peer(step + 1)
        return pltpu.make_async_remote_copy(
            send2.at[peer], recv2.at[me], h2_send.at[step], h2_recv.at[step],
            device_id={"frames": peer}, device_id_type=MESH,
        )

    def w_copy(step):
        return pltpu.make_async_remote_copy(
            wo_ref, wall.at[part], w_send.at[step], w_recv.at[step],
            device_id={"heads": head_peer(step + 1)}, device_id_type=MESH,
        )

    def m_copy(step):
        peer = head_peer(step + 1)
        return pltpu.make_async_remote_copy(
            msend.at[peer], mrecv.at[part], m_send.at[step], m_recv.at[step],
            device_id={"heads": peer}, device_id_type=MESH,
        )

    repeat(devices - 1, lambda s: list_copy(s).start())
    repeat(parts - 1, lambda s: w_copy(s).start())
    listing[me] = pairs_ref[...]

    per = 256 // length
    chunks = frames_here // per

    def project(which, target):
        def body(i, carry):
            rows = x_ref[pl.ds(pl.multiple_of(i * 256, 256), 256), :]
            made = jnp.dot(
                rows,
                w_ref[:, which * breadth : (which + 1) * breadth],
                preferred_element_type=jnp.float32,
            )
            target[pl.ds(i * per, per)] = made.astype(jnp.bfloat16).reshape(per, length, breadth)
            return carry

        lax.fori_loop(0, chunks, body, 0)

    project(1, k_ref)
    project(2, v_ref)

    repeat(devices - 1, lambda s: list_copy(s).wait())
    to_scalar = pltpu.make_async_copy(listing, listing_s, local_sem)
    to_scalar.start()
    to_scalar.wait()

    def mine(owner):
        low = me * frames_here
        frame = jnp.int32(0)
        live = jnp.int32(-1)
        for entry in range(2 * cap):
            value = listing_s[owner, 0, entry]
            hit = (value >= low) & (value < low + frames_here)
            frame = jnp.where(hit, value - low, frame)
            live = jnp.where(hit, value - low, live)
        return frame, live

    def gather(owner):
        frame, _ = mine(owner)
        send1[owner, 0] = k_ref[frame]
        send1[owner, 1] = v_ref[frame]

    repeat(devices, gather)
    repeat(devices - 1, lambda s: hop1(s).start())
    recv1[me] = send1[me]

    project(0, q_ref)

    lane_head = lax.broadcasted_iota(jnp.int32, (length, breadth), 1) // HD

    def attend(queries, key_rows, values):
        stacked = jnp.concatenate(
            [jnp.where(lane_head == h, queries, jnp.zeros_like(queries)) for h in range(heads)],
            axis=0,
        )
        scores = lax.dot_general(
            stacked, key_rows, (((1,), (1,)), ((), ())), preferred_element_type=jnp.float32
        ) * (HD ** -0.5)
        peak = jnp.max(scores, axis=1, keepdims=True)
        lifted = jnp.exp(scores - peak)
        total = jnp.sum(lifted, axis=1, keepdims=True)
        weighted = jnp.dot(
            lifted.astype(jnp.bfloat16), values, preferred_element_type=jnp.float32
        )

        def pick(array):
            shown = jnp.broadcast_to(array[:length], (length, breadth))
            for h in range(1, heads):
                shown = jnp.where(
                    lane_head == h,
                    jnp.broadcast_to(array[h * length : (h + 1) * length], (length, breadth)),
                    shown,
                )
            return shown

        return pick(weighted), pick(peak), pick(total)

    def self_body(f, carry):
        o, m, l = attend(q_ref[f], k_ref[f], v_ref[f])
        so[f] = o
        sm[f] = m
        sl[f] = l
        return carry

    lax.fori_loop(0, frames_here, self_body, 0)

    repeat(devices - 1, lambda s: hop1(s).wait())

    def relay(dest):
        low = dest * frames_here
        partner = me
        for row in range(cap):
            a = listing_s[me, 0, 2 * row]
            b = listing_s[me, 0, 2 * row + 1]
            hit_a = (a >= low) & (a < low + frames_here)
            hit_b = (b >= low) & (b < low + frames_here)
            partner = jnp.where(hit_a, lax.div(b, jnp.int32(frames_here)), partner)
            partner = jnp.where(hit_b, lax.div(a, jnp.int32(frames_here)), partner)
        send2[dest] = recv1[partner]

    repeat(devices, relay)
    repeat(devices - 1, lambda s: hop2(s).start())
    recv2[me] = send2[me]
    repeat(devices - 1, lambda s: hop2(s).wait())

    def pair_body(owner, carry):
        frame, _ = mine(owner)
        o, m, l = attend(q_ref[frame], recv2[owner, 0], recv2[owner, 1])
        po[owner] = o
        pm[owner] = m
        psum[owner] = l
        return carry

    lax.fori_loop(0, devices, pair_body, 0)

    def merge_body(f, carry):
        def raise_peak(owner, top):
            _, live = mine(owner)
            return jnp.maximum(top, jnp.where(live == f, pm[owner], -jnp.inf))

        top = lax.fori_loop(0, devices, raise_peak, sm[f])
        weight = jnp.exp(sm[f] - top)

        def add(owner, state):
            num, den = state
            _, live = mine(owner)
            w = jnp.where(live == f, jnp.exp(pm[owner] - top), 0.0)
            w = jnp.where(live == f, w, 0.0)
            return num + w * po[owner], den + w * psum[owner]

        num, den = lax.fori_loop(0, devices, add, (weight * so[f], weight * sl[f]))
        merged = (num / den).astype(jnp.bfloat16)
        for h in range(parts):
            msend[h, f] = merged[h * share : (h + 1) * share]
        return carry

    lax.fori_loop(0, frames_here, merge_body, 0)

    repeat(parts - 1, lambda s: m_copy(s).start())
    mrecv[part] = msend[part]
    wall[part] = wo_ref[...]
    repeat(parts - 1, lambda s: w_copy(s).wait())
    repeat(parts - 1, lambda s: m_copy(s).wait())
    total = jnp.zeros((frames_here * share, width), jnp.float32)
    for h in range(parts):
        total = total + jnp.dot(
            mrecv[h].reshape(frames_here * share, breadth),
            wall[h],
            preferred_element_type=jnp.float32,
        )
    out_ref[...] = total.astype(jnp.bfloat16).reshape(frames_here, share, width)


def local(tokens, w_qkv, w_out, pair_slots):
    frames_here, length, width = tokens.shape
    breadth = w_qkv.shape[2]
    devices = lax.axis_size("frames")
    parts = lax.axis_size("heads")
    cap = pair_slots.shape[0]
    share = length // parts
    pairs = jnp.zeros((8, 128), jnp.int32).at[0, : 2 * cap].set(pair_slots.reshape(-1))
    bf, f32 = jnp.bfloat16, jnp.float32
    vm = pl.BlockSpec(memory_space=pltpu.VMEM)
    dma = pltpu.SemaphoreType.DMA
    return pl.pallas_call(
        functools.partial(kernel, devices, parts, cap),
        out_shape=jax.ShapeDtypeStruct((frames_here, share, width), bf),
        in_specs=[vm] * 4,
        out_specs=vm,
        scratch_shapes=[
            pltpu.VMEM((devices, 8, 128), jnp.int32),
            pltpu.SMEM((devices, 8, 128), jnp.int32),
            pltpu.VMEM((frames_here, length, breadth), bf),
            pltpu.VMEM((frames_here, length, breadth), bf),
            pltpu.VMEM((frames_here, length, breadth), bf),
        ]
        + [pltpu.VMEM((devices, 2, length, breadth), bf)] * 4
        + [pltpu.VMEM((frames_here, length, breadth), f32)] * 3
        + [pltpu.VMEM((devices, length, breadth), f32)] * 3
        + [
            pltpu.VMEM((parts, frames_here, share, breadth), bf),
            pltpu.VMEM((parts, frames_here, share, breadth), bf),
            pltpu.VMEM((parts, breadth, width), bf),
            dma((devices - 1,)),
            dma((devices - 1,)),
            dma,
        ]
        + [dma((devices - 1,))] * 4
        + [dma((parts - 1,))] * 4,
        compiler_params=pltpu.CompilerParams(
            collective_id=0, has_side_effects=True, vmem_limit_bytes=56 * 1024 * 1024
        ),
    )(
        pairs,
        tokens.reshape(frames_here * length, width),
        w_qkv.reshape(width, 3 * breadth),
        w_out,
    )


def solution(mesh):
    placed = (
        P(("groups", "frames"), None, None),
        P(None, None, "heads"),
        P("heads", None),
        P(("groups", "frames"), None),
    )
    return jax.shard_map(
        local,
        mesh=mesh,
        in_specs=placed,
        out_specs=P(("groups", "frames"), "heads", None),
        check_vma=False,
    )
```

```python
import functools

import jax
import jax.numpy as jnp
from jax import lax
from jax.experimental import pallas as pl
from jax.experimental.pallas import tpu as pltpu
from jax.sharding import PartitionSpec as P

HD = 64
MESH = pl.DeviceIdType.MESH


def repeat(count, body):
    if count <= 8:
        for step in range(count):
            body(step)
    else:

        def step_body(step, carry):
            body(step)
            return carry

        lax.fori_loop(0, count, step_body, 0)


def kernel(
    devices, parts, cap, groups_out,
    pairs_ref, x_hbm, w_hbm, wo_hbm, out_ref,
    x_ref, w_ref, slots, listing, listing_s, info, q_ref, k_ref, v_ref,
    send1k, send1v, recv1k, recv1v, send2k, send2v, recv2k, recv2v,
    so, sm, sl, top, po, pm, psum, pe, msend, mrecv, wall,
    x_sem, w_sem, wo_sem, list_send, list_recv, local_sem,
    h1k_send, h1k_recv, h1v_send, h1v_recv, h2k_send, h2k_recv, h2v_send, h2v_recv,
    w_send, w_recv, m_send, m_recv,
):
    me = lax.axis_index("frames")
    part = lax.axis_index("heads")
    frames_here, length, breadth = q_ref.shape
    width = x_ref.shape[1]
    heads = breadth // HD
    share = length // parts
    per = 256 // length
    chunks = frames_here // per
    group = frames_here // groups_out

    def frame_peer(step):
        return lax.rem(me + step + 1, devices)

    def head_peer(step):
        return lax.rem(part + step + 1, parts)

    barrier = pltpu.get_barrier_semaphore()

    def greet_frames(step):
        pl.semaphore_signal(
            barrier, inc=1, device_id={"frames": frame_peer(step)}, device_id_type=MESH
        )

    def greet_heads(step):
        pl.semaphore_signal(
            barrier, inc=1, device_id={"heads": head_peer(step)}, device_id_type=MESH
        )

    repeat(devices - 1, greet_frames)
    repeat(parts - 1, greet_heads)

    def x_copy(i):
        rows = pl.ds(i * 256, 256)
        return pltpu.make_async_copy(x_hbm.at[rows], x_ref.at[rows], x_sem.at[i])

    def w_load(which):
        return pltpu.make_async_copy(w_hbm.at[which], w_ref.at[which], w_sem.at[which])

    wo_load = pltpu.make_async_copy(wo_hbm, wall.at[part], wo_sem)
    w_load(1).start()
    for i in range(chunks):
        x_copy(i).start()
    w_load(2).start()
    w_load(0).start()
    wo_load.start()

    slots[...] = jnp.zeros_like(slots)
    slots[: pairs_ref.shape[0], : pairs_ref.shape[1]] = pairs_ref[...]
    listing[me] = slots[...]

    def toward(source, target, sends, recvs):
        def make(step):
            peer = frame_peer(step)
            return pltpu.make_async_remote_copy(
                source.at[peer], target.at[me], sends.at[step], recvs.at[step],
                device_id={"frames": peer}, device_id_type=MESH,
            )

        return make

    hop1k = toward(send1k, recv1k, h1k_send, h1k_recv)
    hop1v = toward(send1v, recv1v, h1v_send, h1v_recv)
    hop2k = toward(send2k, recv2k, h2k_send, h2k_recv)
    hop2v = toward(send2v, recv2v, h2v_send, h2v_recv)

    def list_copy(step):
        return pltpu.make_async_remote_copy(
            slots, listing.at[me], list_send.at[step], list_recv.at[step],
            device_id={"frames": frame_peer(step)}, device_id_type=MESH,
        )

    pairwise = parts == 4
    near = part + 1 - 2 * lax.rem(part, 2)
    across = lax.rem(part + 2, parts)

    def w_copy(step):
        if pairwise:
            block = across if step == 2 else part
            peer = across if step == 0 else near
        else:
            block = part
            peer = head_peer(step)
        return pltpu.make_async_remote_copy(
            wall.at[block], wall.at[block], w_send.at[step], w_recv.at[step],
            device_id={"heads": peer}, device_id_type=MESH,
        )

    def m_copy(g, step):
        peer = head_peer(step)
        return pltpu.make_async_remote_copy(
            msend.at[g, peer], mrecv.at[g, part], m_send.at[g, step], m_recv.at[g, step],
            device_id={"heads": peer}, device_id_type=MESH,
        )

    def project(which, target, first):
        w_load(which).wait()

        def body(i, carry):
            if first:
                x_copy(i).wait()
            rows = x_ref[pl.ds(pl.multiple_of(i * 256, 256), 256), :]
            made = jnp.dot(rows, w_ref[which], preferred_element_type=jnp.float32)
            target[pl.ds(i * per, per)] = made.astype(jnp.bfloat16).reshape(per, length, breadth)
            return carry

        lax.fori_loop(0, chunks, body, 0)

    project(1, k_ref, True)
    pl.semaphore_wait(barrier, devices + parts - 2)
    repeat(devices - 1, lambda s: list_copy(s).start())
    wo_load.wait()
    for s in range(2 if pairwise else parts - 1):
        w_copy(s).start()
    project(2, v_ref, False)

    repeat(devices - 1, lambda s: list_copy(s).wait())
    to_scalar = pltpu.make_async_copy(listing, listing_s, local_sem)
    to_scalar.start()
    to_scalar.wait()

    def gather(owner):
        low = me * frames_here
        frame = jnp.int32(0)
        live = jnp.int32(-1)
        for entry in range(2 * cap):
            value = listing_s[owner, entry // 2, entry % 2]
            hit = (value >= low) & (value < low + frames_here)
            frame = jnp.where(hit, value - low, frame)
            live = jnp.where(hit, value - low, live)
        info[0, owner] = frame
        info[1, owner] = live
        send1k[owner] = k_ref[frame]
        send1v[owner] = v_ref[frame]

    repeat(devices, gather)
    repeat(devices - 1, lambda s: hop1k(s).start())
    repeat(devices - 1, lambda s: hop1v(s).start())
    recv1k[me] = send1k[me]
    recv1v[me] = send1v[me]

    project(0, q_ref, False)

    lane_head = lax.broadcasted_iota(jnp.int32, (length, breadth), 1) // HD

    def pick(array):
        shown = jnp.broadcast_to(array[:length], (length, breadth))
        for h in range(1, heads):
            shown = jnp.where(
                lane_head == h,
                jnp.broadcast_to(array[h * length : (h + 1) * length], (length, breadth)),
                shown,
            )
        return shown

    def lift(queries, key_rows):
        stacked = jnp.concatenate(
            [jnp.where(lane_head == h, queries, jnp.zeros_like(queries)) for h in range(heads)],
            axis=0,
        )
        scores = lax.dot_general(
            stacked, key_rows, (((1,), (1,)), ((), ())), preferred_element_type=jnp.float32
        ) * (HD ** -0.5)
        peak = jnp.max(scores, axis=1, keepdims=True)
        lifted = jnp.exp(scores - peak)
        total = jnp.sum(lifted, axis=1, keepdims=True)
        return lifted.astype(jnp.bfloat16), pick(peak), pick(total)

    def self_body(f, carry):
        e, m, l = lift(q_ref[f], k_ref[f])
        so[f] = pick(jnp.dot(e, v_ref[f], preferred_element_type=jnp.float32))
        sm[f] = m
        sl[f] = l
        return carry

    half = frames_here // 2
    lax.fori_loop(0, half, self_body, 0)

    def relay(source, target):
        def body(dest):
            low = dest * frames_here
            partner = me
            for row in range(cap):
                a = listing_s[me, row, 0]
                b = listing_s[me, row, 1]
                hit_a = (a >= low) & (a < low + frames_here)
                hit_b = (b >= low) & (b < low + frames_here)
                partner = jnp.where(hit_a, lax.div(b, jnp.int32(frames_here)), partner)
                partner = jnp.where(hit_b, lax.div(a, jnp.int32(frames_here)), partner)
            target[dest] = source[partner]

        return body

    repeat(devices - 1, lambda s: hop1k(s).wait())
    repeat(devices, relay(recv1k, send2k))
    repeat(devices - 1, lambda s: hop2k(s).start())
    recv2k[me] = send2k[me]

    lax.fori_loop(half, frames_here, self_body, 0)

    repeat(devices - 1, lambda s: hop1v(s).wait())
    repeat(devices, relay(recv1v, send2v))
    repeat(devices - 1, lambda s: hop2v(s).start())
    recv2v[me] = send2v[me]
    if pairwise:
        w_copy(0).wait()
        w_copy(2).start()

    def pair_scores(owner):
        e, m, l = lift(q_ref[info[0, owner]], recv2k[owner])
        pe[owner] = e
        pm[owner] = m
        psum[owner] = l

    def source_of(step):
        return lax.rem(me + devices - step - 1, devices)

    def arrived_scores(step):
        hop2k(step).wait()
        pair_scores(source_of(step))

    pair_scores(me)
    repeat(devices - 1, arrived_scores)

    def peak_body(f, carry):
        def raise_peak(owner, peak):
            return jnp.maximum(peak, jnp.where(info[1, owner] == f, pm[owner], -jnp.inf))

        peak = lax.fori_loop(0, devices, raise_peak, sm[f], unroll=devices <= 8)
        top[f] = peak
        weight = jnp.exp(sm[f] - peak)
        sm[f] = weight
        sl[f] = weight * sl[f]
        return carry

    lax.fori_loop(0, frames_here, peak_body, 0)

    def pair_weight(owner):
        live = info[1, owner] >= 0
        weight = jnp.where(live, jnp.exp(pm[owner] - top[info[0, owner]]), 0.0)
        weight = jnp.where(live, weight, 0.0)
        pm[owner] = weight
        psum[owner] = weight * psum[owner]

    repeat(devices, pair_weight)

    def den_body(f, carry):
        def add(owner, den):
            return den + jnp.where(info[1, owner] == f, psum[owner], 0.0)

        den = lax.fori_loop(0, devices, add, sl[f], unroll=devices <= 8)
        inverse = 1.0 / den
        top[f] = inverse
        so[f] = so[f] * (sm[f] * inverse)
        return carry

    lax.fori_loop(0, frames_here, den_body, 0)

    def pair_values(owner):
        made = jnp.dot(pe[owner], recv2v[owner], preferred_element_type=jnp.float32)
        po[owner] = pick(made) * (pm[owner] * top[info[0, owner]])

    def arrived_values(step):
        hop2v(step).wait()
        pair_values(source_of(step))

    pair_values(me)
    repeat(devices - 1, arrived_values)

    for g in range(groups_out):

        def merge_body(i, carry):
            f = g * group + i

            def add(owner, state):
                return state + jnp.where(info[1, owner] == f, po[owner], 0.0)

            merged = lax.fori_loop(0, devices, add, so[f], unroll=devices <= 8)
            merged = merged.astype(jnp.bfloat16)
            for h in range(parts):
                msend[g, h, i] = merged[h * share : (h + 1) * share]
            return carry

        lax.fori_loop(0, group, merge_body, 0)
        for s in range(parts - 1):
            m_copy(g, s).start()
        mrecv[g, part] = msend[g, part]

    for s in range(1 if pairwise else 0, parts - 1):
        w_copy(s).wait()
    for g in range(groups_out):
        for s in range(parts - 1):
            m_copy(g, s).wait()
        total = jnp.zeros((group * share, width), jnp.float32)
        for h in range(parts):
            total = total + jnp.dot(
                mrecv[g, h].reshape(group * share, breadth),
                wall[h],
                preferred_element_type=jnp.float32,
            )
        out_ref[pl.ds(g * group, group)] = total.astype(jnp.bfloat16).reshape(
            group, share, width
        )


def local(tokens, w_qkv, w_out, pair_slots):
    frames_here, length, width = tokens.shape
    breadth = w_qkv.shape[2]
    devices = lax.axis_size("frames")
    parts = lax.axis_size("heads")
    cap = pair_slots.shape[0]
    share = length // parts
    rows = -(-cap // 8) * 8
    groups_out = 2
    group = frames_here // groups_out
    bf, f32 = jnp.bfloat16, jnp.float32
    vm = pl.BlockSpec(memory_space=pltpu.VMEM)
    hbm = pl.BlockSpec(memory_space=pl.ANY)
    dma = pltpu.SemaphoreType.DMA
    frame_bf = pltpu.VMEM((frames_here, length, breadth), bf)
    frame_f = pltpu.VMEM((frames_here, length, breadth), f32)
    slot_bf = pltpu.VMEM((devices, length, breadth), bf)
    slot_f = pltpu.VMEM((devices, length, breadth), f32)
    return pl.pallas_call(
        functools.partial(kernel, devices, parts, cap, groups_out),
        out_shape=jax.ShapeDtypeStruct((frames_here, share, width), bf),
        in_specs=[vm, hbm, hbm, hbm],
        out_specs=vm,
        scratch_shapes=[
            pltpu.VMEM((frames_here * length, width), bf),
            pltpu.VMEM((3, width, breadth), bf),
            pltpu.VMEM((rows, 128), jnp.int32),
            pltpu.VMEM((devices, rows, 128), jnp.int32),
            pltpu.SMEM((devices, rows, 128), jnp.int32),
            pltpu.SMEM((2, devices), jnp.int32),
        ]
        + [frame_bf] * 3
        + [slot_bf] * 8
        + [frame_f] * 4
        + [slot_f] * 3
        + [
            pltpu.VMEM((devices, length * (breadth // HD), length), bf),
            pltpu.VMEM((groups_out, parts, group, share, breadth), bf),
            pltpu.VMEM((groups_out, parts, group, share, breadth), bf),
            pltpu.VMEM((parts, breadth, width), bf),
            dma((frames_here * length // 256,)),
            dma((3,)),
            dma,
            dma((devices - 1,)),
            dma((devices - 1,)),
            dma,
        ]
        + [dma((devices - 1,))] * 8
        + [dma((parts - 1,))] * 2
        + [dma((groups_out, parts - 1))] * 2,
        compiler_params=pltpu.CompilerParams(
            collective_id=0, has_side_effects=True, vmem_limit_bytes=60 * 1024 * 1024
        ),
    )(
        pair_slots,
        tokens.reshape(frames_here * length, width),
        jnp.transpose(w_qkv, (1, 0, 2)),
        w_out,
    )


def solution(mesh):
    placed = (
        P(("groups", "frames"), None, None),
        P(None, None, "heads"),
        P("heads", None),
        P(("groups", "frames"), None),
    )
    return jax.shard_map(
        local,
        mesh=mesh,
        in_specs=placed,
        out_specs=P(("groups", "frames"), "heads", None),
        check_vma=False,
    )
```

```python
import functools

import jax
import jax.numpy as jnp
from jax import lax
from jax.experimental import pallas as pl
from jax.experimental.pallas import tpu as pltpu
from jax.sharding import PartitionSpec as P

HD = 64
MESH = pl.DeviceIdType.MESH


def repeat(count, body):
    if count <= 8:
        for step in range(count):
            body(step)
    else:

        def step_body(step, carry):
            body(step)
            return carry

        lax.fori_loop(0, count, step_body, 0)


def kernel(
    devices, parts, cap, groups_out,
    pairs_ref, x_hbm, w_hbm, wo_hbm, out_ref,
    x_ref, w_ref, slots, listing, listing_s, info, q_ref, k_ref, v_ref,
    send1, recv1, send2, xs,
    so, sm, sl, top, po, pm, psum, msend, mrecv, wall,
    x_sem, w_sem, wo_sem, list_send, list_recv, local_sem,
    h1_send, h1_recv, h2_send, h2_recv, g_send, g_recv,
    w_send, w_recv, m_send, m_recv,
):
    me = lax.axis_index("frames")
    part = lax.axis_index("heads")
    frames_here, length, breadth = q_ref.shape
    width = x_ref.shape[2]
    heads = breadth // HD
    share = length // parts
    per = 256 // length
    chunks = frames_here // per
    group = frames_here // groups_out

    def frame_peer(step):
        return lax.rem(me + step + 1, devices)

    def head_peer(step):
        return lax.rem(part + step + 1, parts)

    barrier = pltpu.get_barrier_semaphore()

    def greet_frames(step):
        pl.semaphore_signal(
            barrier, inc=1, device_id={"frames": frame_peer(step)}, device_id_type=MESH
        )

    def greet_heads(step):
        pl.semaphore_signal(
            barrier, inc=1, device_id={"heads": head_peer(step)}, device_id_type=MESH
        )

    repeat(devices - 1, greet_frames)
    repeat(parts - 1, greet_heads)

    def x_copy(i):
        rows = pl.ds(i * per, per)
        return pltpu.make_async_copy(x_hbm.at[rows], x_ref.at[rows], x_sem.at[i])

    def w_load(which):
        return pltpu.make_async_copy(w_hbm.at[which], w_ref.at[which], w_sem.at[which])

    wo_load = pltpu.make_async_copy(wo_hbm, wall.at[part], wo_sem)
    w_load(1).start()
    for i in range(chunks):
        x_copy(i).start()
    w_load(2).start()
    w_load(0).start()
    wo_load.start()

    slots[...] = jnp.zeros_like(slots)
    slots[: pairs_ref.shape[0], : pairs_ref.shape[1]] = pairs_ref[...]
    listing[me] = slots[...]

    def own_rows(block):
        return pl.ds(pl.multiple_of(block * share, share), share)

    def hop1(step):
        peer = frame_peer(step)
        return pltpu.make_async_remote_copy(
            send1.at[peer], recv1.at[me], h1_send.at[step], h1_recv.at[step],
            device_id={"frames": peer}, device_id_type=MESH,
        )

    def hop2(step):
        peer = frame_peer(step)
        return pltpu.make_async_remote_copy(
            send2.at[peer], xs.at[me, own_rows(part)], h2_send.at[step], h2_recv.at[step],
            device_id={"frames": peer}, device_id_type=MESH,
        )

    def list_copy(step):
        return pltpu.make_async_remote_copy(
            slots, listing.at[me], list_send.at[step], list_recv.at[step],
            device_id={"frames": frame_peer(step)}, device_id_type=MESH,
        )

    pairwise = parts == 4
    near = part + 1 - 2 * lax.rem(part, 2)
    across = lax.rem(part + 2, parts)

    def w_copy(step):
        if pairwise:
            block = across if step == 2 else part
            peer = across if step == 0 else near
        else:
            block = part
            peer = head_peer(step)
        return pltpu.make_async_remote_copy(
            wall.at[block], wall.at[block], w_send.at[step], w_recv.at[step],
            device_id={"heads": peer}, device_id_type=MESH,
        )

    def slot_of(k):
        return lax.rem(me + devices - k, devices)

    def g_copy(k, step):
        if pairwise:
            block = across if step == 2 else part
            peer = across if step == 0 else near
        else:
            block = part
            peer = head_peer(step)
        piece = xs.at[slot_of(k), own_rows(block)]
        return pltpu.make_async_remote_copy(
            piece, piece, g_send.at[k, step], g_recv.at[k, step],
            device_id={"heads": peer}, device_id_type=MESH,
        )

    def spread(k):
        for step in range(2 if pairwise else parts - 1):
            g_copy(k, step).start()

    def forward(k):
        if pairwise:
            g_copy(k, 0).wait()
            g_copy(k, 2).start()

    def collect(k):
        for step in range(1 if pairwise else 0, parts - 1):
            g_copy(k, step).wait()

    def m_copy(g, step):
        peer = head_peer(step)
        return pltpu.make_async_remote_copy(
            msend.at[g, peer], mrecv.at[g, part], m_send.at[g, step], m_recv.at[g, step],
            device_id={"heads": peer}, device_id_type=MESH,
        )

    def project(which, target, first):
        w_load(which).wait()

        def body(i, carry):
            if first:
                x_copy(i).wait()
            rows = x_ref[pl.ds(i * per, per)].reshape(per * length, width)
            made = jnp.dot(rows, w_ref[which], preferred_element_type=jnp.float32)
            target[pl.ds(i * per, per)] = made.astype(jnp.bfloat16).reshape(per, length, breadth)
            return carry

        lax.fori_loop(0, chunks, body, 0)

    project(1, k_ref, True)
    pl.semaphore_wait(barrier, devices + parts - 2)
    repeat(devices - 1, lambda s: list_copy(s).start())
    wo_load.wait()
    for s in range(2 if pairwise else parts - 1):
        w_copy(s).start()
    repeat(devices - 1, lambda s: list_copy(s).wait())
    to_scalar = pltpu.make_async_copy(listing, listing_s, local_sem)
    to_scalar.start()
    to_scalar.wait()

    def gather(owner):
        low = me * frames_here
        frame = jnp.int32(0)
        live = jnp.int32(-1)
        for entry in range(2 * cap):
            value = listing_s[owner, entry // 2, entry % 2]
            hit = (value >= low) & (value < low + frames_here)
            frame = jnp.where(hit, value - low, frame)
            live = jnp.where(hit, value - low, live)
        info[0, owner] = frame
        info[1, owner] = live
        send1[owner] = x_ref[frame, own_rows(part)]

    repeat(devices, gather)
    repeat(devices - 1, lambda s: hop1(s).start())
    recv1[me] = send1[me]

    project(2, v_ref, False)
    project(0, q_ref, False)

    lane_head = lax.broadcasted_iota(jnp.int32, (length, breadth), 1) // HD

    def pick(array):
        shown = jnp.broadcast_to(array[:length], (length, breadth))
        for h in range(1, heads):
            shown = jnp.where(
                lane_head == h,
                jnp.broadcast_to(array[h * length : (h + 1) * length], (length, breadth)),
                shown,
            )
        return shown

    def lift(queries, key_rows):
        stacked = jnp.concatenate(
            [jnp.where(lane_head == h, queries, jnp.zeros_like(queries)) for h in range(heads)],
            axis=0,
        )
        scores = lax.dot_general(
            stacked, key_rows, (((1,), (1,)), ((), ())), preferred_element_type=jnp.float32
        ) * (HD ** -0.5)
        peak = jnp.max(scores, axis=1, keepdims=True)
        lifted = jnp.exp(scores - peak)
        total = jnp.sum(lifted, axis=1, keepdims=True)
        return lifted.astype(jnp.bfloat16), pick(peak), pick(total)

    def self_body(f, carry):
        e, m, l = lift(q_ref[f], k_ref[f])
        so[f] = pick(jnp.dot(e, v_ref[f], preferred_element_type=jnp.float32))
        sm[f] = m
        sl[f] = l
        return carry

    half = frames_here // 2
    lax.fori_loop(0, half, self_body, 0)

    def relay(dest):
        low = dest * frames_here
        partner = me
        for row in range(cap):
            a = listing_s[me, row, 0]
            b = listing_s[me, row, 1]
            hit_a = (a >= low) & (a < low + frames_here)
            hit_b = (b >= low) & (b < low + frames_here)
            partner = jnp.where(hit_a, lax.div(b, jnp.int32(frames_here)), partner)
            partner = jnp.where(hit_b, lax.div(a, jnp.int32(frames_here)), partner)
        send2[dest] = recv1[partner]

    repeat(devices - 1, lambda s: hop1(s).wait())
    repeat(devices, relay)
    repeat(devices - 1, lambda s: hop2(s).start())
    xs[me, own_rows(part)] = send2[me]
    spread(0)
    if pairwise:
        w_copy(0).wait()
        w_copy(2).start()

    lax.fori_loop(half, frames_here, self_body, 0)
    forward(0)

    def pair_attend(k):
        owner = slot_of(k)
        rows = xs[owner]
        keys = jnp.dot(rows, w_ref[1], preferred_element_type=jnp.float32).astype(jnp.bfloat16)
        values = jnp.dot(rows, w_ref[2], preferred_element_type=jnp.float32).astype(jnp.bfloat16)
        e, m, l = lift(q_ref[info[0, owner]], keys)
        po[owner] = pick(jnp.dot(e, values, preferred_element_type=jnp.float32))
        pm[owner] = m
        psum[owner] = l

    def arrived(step):
        hop2(step).wait()
        spread(step + 1)
        collect(step)
        pair_attend(step)
        forward(step + 1)

    repeat(devices - 1, arrived)
    collect(devices - 1)
    pair_attend(devices - 1)

    def peak_body(f, carry):
        def raise_peak(owner, peak):
            return jnp.maximum(peak, jnp.where(info[1, owner] == f, pm[owner], -jnp.inf))

        peak = lax.fori_loop(0, devices, raise_peak, sm[f], unroll=devices <= 8)
        top[f] = peak
        weight = jnp.exp(sm[f] - peak)
        sm[f] = weight
        sl[f] = weight * sl[f]
        return carry

    lax.fori_loop(0, frames_here, peak_body, 0)

    def pair_weight(owner):
        live = info[1, owner] >= 0
        weight = jnp.where(live, jnp.exp(pm[owner] - top[info[0, owner]]), 0.0)
        weight = jnp.where(live, weight, 0.0)
        pm[owner] = weight
        psum[owner] = weight * psum[owner]

    repeat(devices, pair_weight)

    def den_body(f, carry):
        def add(owner, den):
            return den + jnp.where(info[1, owner] == f, psum[owner], 0.0)

        den = lax.fori_loop(0, devices, add, sl[f], unroll=devices <= 8)
        inverse = 1.0 / den
        top[f] = inverse
        so[f] = so[f] * (sm[f] * inverse)
        return carry

    lax.fori_loop(0, frames_here, den_body, 0)

    def pair_scale(owner):
        po[owner] = po[owner] * (pm[owner] * top[info[0, owner]])

    repeat(devices, pair_scale)

    for g in range(groups_out):

        def merge_body(i, carry):
            f = g * group + i

            def add(owner, state):
                return state + jnp.where(info[1, owner] == f, po[owner], 0.0)

            merged = lax.fori_loop(0, devices, add, so[f], unroll=devices <= 8)
            merged = merged.astype(jnp.bfloat16)
            for h in range(parts):
                msend[g, h, i] = merged[h * share : (h + 1) * share]
            return carry

        lax.fori_loop(0, group, merge_body, 0)
        for s in range(parts - 1):
            m_copy(g, s).start()
        mrecv[g, part] = msend[g, part]

    for s in range(1 if pairwise else 0, parts - 1):
        w_copy(s).wait()
    for g in range(groups_out):
        for s in range(parts - 1):
            m_copy(g, s).wait()
        total = jnp.zeros((group * share, width), jnp.float32)
        for h in range(parts):
            total = total + jnp.dot(
                mrecv[g, h].reshape(group * share, breadth),
                wall[h],
                preferred_element_type=jnp.float32,
            )
        out_ref[pl.ds(g * group, group)] = total.astype(jnp.bfloat16).reshape(
            group, share, width
        )


def local(tokens, w_qkv, w_out, pair_slots):
    frames_here, length, width = tokens.shape
    breadth = w_qkv.shape[2]
    devices = lax.axis_size("frames")
    parts = lax.axis_size("heads")
    cap = pair_slots.shape[0]
    share = length // parts
    rows = -(-cap // 8) * 8
    groups_out = 2
    group = frames_here // groups_out
    bf, f32 = jnp.bfloat16, jnp.float32
    vm = pl.BlockSpec(memory_space=pltpu.VMEM)
    hbm = pl.BlockSpec(memory_space=pl.ANY)
    dma = pltpu.SemaphoreType.DMA
    frame_bf = pltpu.VMEM((frames_here, length, breadth), bf)
    frame_f = pltpu.VMEM((frames_here, length, breadth), f32)
    slot_bf = pltpu.VMEM((devices, share, width), bf)
    slot_f = pltpu.VMEM((devices, length, breadth), f32)
    return pl.pallas_call(
        functools.partial(kernel, devices, parts, cap, groups_out),
        out_shape=jax.ShapeDtypeStruct((frames_here, share, width), bf),
        in_specs=[vm, hbm, hbm, hbm],
        out_specs=vm,
        scratch_shapes=[
            pltpu.VMEM((frames_here, length, width), bf),
            pltpu.VMEM((3, width, breadth), bf),
            pltpu.VMEM((rows, 128), jnp.int32),
            pltpu.VMEM((devices, rows, 128), jnp.int32),
            pltpu.SMEM((devices, rows, 128), jnp.int32),
            pltpu.SMEM((2, devices), jnp.int32),
        ]
        + [frame_bf] * 3
        + [slot_bf] * 3
        + [pltpu.VMEM((devices, length, width), bf)]
        + [frame_f] * 4
        + [slot_f] * 3
        + [
            pltpu.VMEM((groups_out, parts, group, share, breadth), bf),
            pltpu.VMEM((groups_out, parts, group, share, breadth), bf),
            pltpu.VMEM((parts, breadth, width), bf),
            dma((frames_here * length // 256,)),
            dma((3,)),
            dma,
            dma((devices - 1,)),
            dma((devices - 1,)),
            dma,
        ]
        + [dma((devices - 1,))] * 4
        + [dma((devices, parts - 1))] * 2
        + [dma((parts - 1,))] * 2
        + [dma((groups_out, parts - 1))] * 2,
        compiler_params=pltpu.CompilerParams(
            collective_id=0, has_side_effects=True, vmem_limit_bytes=60 * 1024 * 1024
        ),
    )(
        pair_slots,
        tokens,
        jnp.transpose(w_qkv, (1, 0, 2)),
        w_out,
    )


def solution(mesh):
    placed = (
        P(("groups", "frames"), None, None),
        P(None, None, "heads"),
        P("heads", None),
        P(("groups", "frames"), None),
    )
    return jax.shard_map(
        local,
        mesh=mesh,
        in_specs=placed,
        out_specs=P(("groups", "frames"), "heads", None),
        check_vma=False,
    )
```

```python
import functools

import jax
import jax.numpy as jnp
from jax import lax
from jax.experimental import pallas as pl
from jax.experimental.pallas import tpu as pltpu
from jax.sharding import PartitionSpec as P

HD = 64
MESH = pl.DeviceIdType.MESH


def repeat(count, body):
    if count <= 8:
        for step in range(count):
            body(step)
    else:

        def step_body(step, carry):
            body(step)
            return carry

        lax.fori_loop(0, count, step_body, 0)


def kernel(
    devices, parts, cap, groups_out,
    pairs_ref, x_hbm, w_hbm, wo_hbm, out_ref,
    x_ref, w_ref, slots, listing, listing_s, info, q_ref, k_ref, v_ref,
    send1, recv1, send2, xs,
    so, sm, sl, top, po, pm, psum, msend, mrecv, wall,
    x_sem, w_sem, wo_sem, list_send, list_recv, local_sem,
    h1_send, h1_recv, h2_send, h2_recv, g_send, g_recv,
    w_send, w_recv, m_send, m_recv,
):
    me = lax.axis_index("frames")
    part = lax.axis_index("heads")
    frames_here, length, breadth = q_ref.shape
    width = x_ref.shape[2]
    heads = breadth // HD
    share = length // parts
    per = 256 // length
    chunks = frames_here // per
    group = frames_here // groups_out

    def frame_peer(step):
        return lax.rem(me + step + 1, devices)

    def head_peer(step):
        return lax.rem(part + step + 1, parts)

    barrier = pltpu.get_barrier_semaphore()

    def greet_frames(step):
        pl.semaphore_signal(
            barrier, inc=1, device_id={"frames": frame_peer(step)}, device_id_type=MESH
        )

    def greet_heads(step):
        pl.semaphore_signal(
            barrier, inc=1, device_id={"heads": head_peer(step)}, device_id_type=MESH
        )

    repeat(devices - 1, greet_frames)
    repeat(parts - 1, greet_heads)

    def x_copy(i):
        rows = pl.ds(i * per, per)
        return pltpu.make_async_copy(x_hbm.at[rows], x_ref.at[rows], x_sem.at[i])

    def w_load(which):
        return pltpu.make_async_copy(w_hbm.at[which], w_ref.at[which], w_sem.at[which])

    wo_load = pltpu.make_async_copy(wo_hbm, wall.at[part], wo_sem)
    w_load(1).start()
    for i in range(chunks):
        x_copy(i).start()
    w_load(2).start()
    w_load(0).start()
    wo_load.start()

    slots[...] = jnp.zeros_like(slots)
    slots[: pairs_ref.shape[0], : pairs_ref.shape[1]] = pairs_ref[...]
    listing[me] = slots[...]

    def own_rows(block):
        return pl.ds(pl.multiple_of(block * share, share), share)

    def hop1(step):
        peer = frame_peer(step)
        return pltpu.make_async_remote_copy(
            send1.at[peer], recv1.at[me], h1_send.at[step], h1_recv.at[step],
            device_id={"frames": peer}, device_id_type=MESH,
        )

    def hop2(step):
        peer = frame_peer(step)
        return pltpu.make_async_remote_copy(
            send2.at[peer], xs.at[me, own_rows(part)], h2_send.at[step], h2_recv.at[step],
            device_id={"frames": peer}, device_id_type=MESH,
        )

    def list_copy(step):
        return pltpu.make_async_remote_copy(
            slots, listing.at[me], list_send.at[step], list_recv.at[step],
            device_id={"frames": frame_peer(step)}, device_id_type=MESH,
        )

    pairwise = parts == 4
    near = part + 1 - 2 * lax.rem(part, 2)
    across = lax.rem(part + 2, parts)

    def w_copy(step):
        if pairwise:
            block = across if step == 2 else part
            peer = across if step == 0 else near
        else:
            block = part
            peer = head_peer(step)
        return pltpu.make_async_remote_copy(
            wall.at[block], wall.at[block], w_send.at[step], w_recv.at[step],
            device_id={"heads": peer}, device_id_type=MESH,
        )

    def slot_of(k):
        return lax.rem(me + devices - k, devices)

    def g_copy(k, step):
        block = part
        peer = head_peer(step)
        piece = xs.at[slot_of(k), own_rows(block)]
        return pltpu.make_async_remote_copy(
            piece, piece, g_send.at[k, step], g_recv.at[k, step],
            device_id={"heads": peer}, device_id_type=MESH,
        )

    def spread(k):
        for step in range(parts - 1):
            g_copy(k, step).start()

    def collect(k):
        for step in range(parts - 1):
            g_copy(k, step).wait()

    def m_copy(g, step):
        peer = head_peer(step)
        return pltpu.make_async_remote_copy(
            msend.at[g, peer], mrecv.at[g, part], m_send.at[g, step], m_recv.at[g, step],
            device_id={"heads": peer}, device_id_type=MESH,
        )

    def project(which, target, first):
        w_load(which).wait()

        def body(i, carry):
            if first:
                x_copy(i).wait()
            rows = x_ref[pl.ds(i * per, per)].reshape(per * length, width)
            made = jnp.dot(rows, w_ref[which], preferred_element_type=jnp.float32)
            target[pl.ds(i * per, per)] = made.astype(jnp.bfloat16).reshape(per, length, breadth)
            return carry

        lax.fori_loop(0, chunks, body, 0)

    project(1, k_ref, True)
    pl.semaphore_wait(barrier, devices + parts - 2)
    repeat(devices - 1, lambda s: list_copy(s).start())
    wo_load.wait()
    for s in range(2 if pairwise else parts - 1):
        w_copy(s).start()
    repeat(devices - 1, lambda s: list_copy(s).wait())
    to_scalar = pltpu.make_async_copy(listing, listing_s, local_sem)
    to_scalar.start()
    to_scalar.wait()

    def gather(owner):
        low = me * frames_here
        frame = jnp.int32(0)
        live = jnp.int32(-1)
        for entry in range(2 * cap):
            value = listing_s[owner, entry // 2, entry % 2]
            hit = (value >= low) & (value < low + frames_here)
            frame = jnp.where(hit, value - low, frame)
            live = jnp.where(hit, value - low, live)
        info[0, owner] = frame
        info[1, owner] = live
        send1[owner] = x_ref[frame, own_rows(part)]

    repeat(devices, gather)
    repeat(devices - 1, lambda s: hop1(s).start())
    recv1[me] = send1[me]

    project(2, v_ref, False)
    lane_head = lax.broadcasted_iota(jnp.int32, (length, breadth), 1) // HD

    def pick(array):
        shown = jnp.broadcast_to(array[:length], (length, breadth))
        for h in range(1, heads):
            shown = jnp.where(
                lane_head == h,
                jnp.broadcast_to(array[h * length : (h + 1) * length], (length, breadth)),
                shown,
            )
        return shown

    def lift(queries, key_rows):
        stacked = jnp.concatenate(
            [jnp.where(lane_head == h, queries, jnp.zeros_like(queries)) for h in range(heads)],
            axis=0,
        )
        scores = lax.dot_general(
            stacked, key_rows, (((1,), (1,)), ((), ())), preferred_element_type=jnp.float32
        ) * (HD ** -0.5)
        peak = jnp.max(scores, axis=1, keepdims=True)
        lifted = jnp.exp(scores - peak)
        total = jnp.sum(lifted, axis=1, keepdims=True)
        return lifted.astype(jnp.bfloat16), pick(peak), pick(total)

    def self_body(f, carry):
        e, m, l = lift(q_ref[f], k_ref[f])
        so[f] = pick(jnp.dot(e, v_ref[f], preferred_element_type=jnp.float32))
        sm[f] = m
        sl[f] = l
        return carry

    def relay(dest):
        low = dest * frames_here
        partner = me
        for row in range(cap):
            a = listing_s[me, row, 0]
            b = listing_s[me, row, 1]
            hit_a = (a >= low) & (a < low + frames_here)
            hit_b = (b >= low) & (b < low + frames_here)
            partner = jnp.where(hit_a, lax.div(b, jnp.int32(frames_here)), partner)
            partner = jnp.where(hit_b, lax.div(a, jnp.int32(frames_here)), partner)
        send2[dest] = recv1[partner]

    repeat(devices - 1, lambda s: hop1(s).wait())
    repeat(devices, relay)
    repeat(devices - 1, lambda s: hop2(s).start())
    xs[me, own_rows(part)] = send2[me]
    spread(0)
    project(0, q_ref, False)

    def pair_attend(k):
        owner = slot_of(k)
        rows = xs[owner]
        keys = jnp.dot(rows, w_ref[1], preferred_element_type=jnp.float32).astype(jnp.bfloat16)
        values = jnp.dot(rows, w_ref[2], preferred_element_type=jnp.float32).astype(jnp.bfloat16)
        e, m, l = lift(q_ref[info[0, owner]], keys)
        po[owner] = pick(jnp.dot(e, values, preferred_element_type=jnp.float32))
        pm[owner] = m
        psum[owner] = l

    def arrived(step):
        hop2(step).wait()
        spread(step + 1)

    def finish(k):
        collect(k)
        pair_attend(k)

    repeat(devices - 1, arrived)
    lax.fori_loop(0, frames_here, self_body, 0)

    finish(0)
    repeat(devices - 1, lambda s: finish(s + 1))

    if pairwise:
        w_copy(0).wait()
        w_copy(2).start()

    def peak_body(f, carry):
        def raise_peak(owner, peak):
            return jnp.maximum(peak, jnp.where(info[1, owner] == f, pm[owner], -jnp.inf))

        peak = lax.fori_loop(0, devices, raise_peak, sm[f], unroll=devices <= 8)
        top[f] = peak
        weight = jnp.exp(sm[f] - peak)
        sm[f] = weight
        sl[f] = weight * sl[f]
        return carry

    lax.fori_loop(0, frames_here, peak_body, 0)

    def pair_weight(owner):
        live = info[1, owner] >= 0
        weight = jnp.where(live, jnp.exp(pm[owner] - top[info[0, owner]]), 0.0)
        weight = jnp.where(live, weight, 0.0)
        pm[owner] = weight
        psum[owner] = weight * psum[owner]

    repeat(devices, pair_weight)

    def den_body(f, carry):
        def add(owner, den):
            return den + jnp.where(info[1, owner] == f, psum[owner], 0.0)

        den = lax.fori_loop(0, devices, add, sl[f], unroll=devices <= 8)
        inverse = 1.0 / den
        top[f] = inverse
        so[f] = so[f] * (sm[f] * inverse)
        return carry

    lax.fori_loop(0, frames_here, den_body, 0)

    def pair_scale(owner):
        po[owner] = po[owner] * (pm[owner] * top[info[0, owner]])

    repeat(devices, pair_scale)

    for g in range(groups_out):

        def merge_body(i, carry):
            f = g * group + i

            def add(owner, state):
                return state + jnp.where(info[1, owner] == f, po[owner], 0.0)

            merged = lax.fori_loop(0, devices, add, so[f], unroll=devices <= 8)
            merged = merged.astype(jnp.bfloat16)
            for h in range(parts):
                msend[g, h, i] = merged[h * share : (h + 1) * share]
            return carry

        lax.fori_loop(0, group, merge_body, 0)
        for s in range(parts - 1):
            m_copy(g, s).start()
        mrecv[g, part] = msend[g, part]

    for s in range(1 if pairwise else 0, parts - 1):
        w_copy(s).wait()
    for g in range(groups_out):
        for s in range(parts - 1):
            m_copy(g, s).wait()
        total = jnp.zeros((group * share, width), jnp.float32)
        for h in range(parts):
            total = total + jnp.dot(
                mrecv[g, h].reshape(group * share, breadth),
                wall[h],
                preferred_element_type=jnp.float32,
            )
        out_ref[pl.ds(g * group, group)] = total.astype(jnp.bfloat16).reshape(
            group, share, width
        )


def local(tokens, w_qkv, w_out, pair_slots):
    frames_here, length, width = tokens.shape
    breadth = w_qkv.shape[2]
    devices = lax.axis_size("frames")
    parts = lax.axis_size("heads")
    cap = pair_slots.shape[0]
    share = length // parts
    rows = -(-cap // 8) * 8
    groups_out = 2
    group = frames_here // groups_out
    bf, f32 = jnp.bfloat16, jnp.float32
    vm = pl.BlockSpec(memory_space=pltpu.VMEM)
    hbm = pl.BlockSpec(memory_space=pl.ANY)
    dma = pltpu.SemaphoreType.DMA
    frame_bf = pltpu.VMEM((frames_here, length, breadth), bf)
    frame_f = pltpu.VMEM((frames_here, length, breadth), f32)
    slot_bf = pltpu.VMEM((devices, share, width), bf)
    slot_f = pltpu.VMEM((devices, length, breadth), f32)
    return pl.pallas_call(
        functools.partial(kernel, devices, parts, cap, groups_out),
        out_shape=jax.ShapeDtypeStruct((frames_here, share, width), bf),
        in_specs=[vm, hbm, hbm, hbm],
        out_specs=vm,
        scratch_shapes=[
            pltpu.VMEM((frames_here, length, width), bf),
            pltpu.VMEM((3, width, breadth), bf),
            pltpu.VMEM((rows, 128), jnp.int32),
            pltpu.VMEM((devices, rows, 128), jnp.int32),
            pltpu.SMEM((devices, rows, 128), jnp.int32),
            pltpu.SMEM((2, devices), jnp.int32),
        ]
        + [frame_bf] * 3
        + [slot_bf] * 3
        + [pltpu.VMEM((devices, length, width), bf)]
        + [frame_f] * 4
        + [slot_f] * 3
        + [
            pltpu.VMEM((groups_out, parts, group, share, breadth), bf),
            pltpu.VMEM((groups_out, parts, group, share, breadth), bf),
            pltpu.VMEM((parts, breadth, width), bf),
            dma((frames_here * length // 256,)),
            dma((3,)),
            dma,
            dma((devices - 1,)),
            dma((devices - 1,)),
            dma,
        ]
        + [dma((devices - 1,))] * 4
        + [dma((devices, parts - 1))] * 2
        + [dma((parts - 1,))] * 2
        + [dma((groups_out, parts - 1))] * 2,
        compiler_params=pltpu.CompilerParams(
            collective_id=0, has_side_effects=True, vmem_limit_bytes=60 * 1024 * 1024
        ),
    )(
        pair_slots,
        tokens,
        jnp.transpose(w_qkv, (1, 0, 2)),
        w_out,
    )


def solution(mesh):
    placed = (
        P(("groups", "frames"), None, None),
        P(None, None, "heads"),
        P("heads", None),
        P(("groups", "frames"), None),
    )
    return jax.shard_map(
        local,
        mesh=mesh,
        in_specs=placed,
        out_specs=P(("groups", "frames"), "heads", None),
        check_vma=False,
    )
```

```python
import functools

import jax
import jax.numpy as jnp
from jax import lax
from jax.experimental import pallas as pl
from jax.experimental.pallas import tpu as pltpu
from jax.sharding import PartitionSpec as P

HD = 64
MESH = pl.DeviceIdType.MESH


def repeat(count, body):
    if count <= 8:
        for step in range(count):
            body(step)
    else:

        def step_body(step, carry):
            body(step)
            return carry

        lax.fori_loop(0, count, step_body, 0)


def kernel(
    devices, parts, cap, groups_out,
    pairs_ref, x_hbm, w_hbm, wo_hbm, out_ref,
    x_ref, w_ref, slots, listing, listing_s, info, q_ref, k_ref, v_ref,
    send1, recv1, send2, xs,
    so, sm, sl, top, po, pm, psum, msend, mrecv, wall,
    x_sem, w_sem, wo_sem, list_send, list_recv, local_sem,
    h1_send, h1_recv, h2_send, h2_recv, g_send, g_recv,
    w_send, w_recv, m_send, m_recv,
):
    me = lax.axis_index("frames")
    part = lax.axis_index("heads")
    frames_here, length, breadth = q_ref.shape
    width = x_ref.shape[2]
    heads = breadth // HD
    share = length // parts
    per = 256 // length
    chunks = frames_here // per
    group = frames_here // groups_out

    def frame_peer(step):
        return lax.rem(me + step + 1, devices)

    def head_peer(step):
        return lax.rem(part + step + 1, parts)

    barrier = pltpu.get_barrier_semaphore()

    def greet_frames(step):
        pl.semaphore_signal(
            barrier, inc=1, device_id={"frames": frame_peer(step)}, device_id_type=MESH
        )

    def greet_heads(step):
        pl.semaphore_signal(
            barrier, inc=1, device_id={"heads": head_peer(step)}, device_id_type=MESH
        )

    repeat(devices - 1, greet_frames)
    repeat(parts - 1, greet_heads)

    def x_copy(i):
        rows = pl.ds(i * per, per)
        return pltpu.make_async_copy(x_hbm.at[rows], x_ref.at[rows], x_sem.at[i])

    def w_load(which):
        return pltpu.make_async_copy(w_hbm.at[which], w_ref.at[which], w_sem.at[which])

    wo_load = pltpu.make_async_copy(wo_hbm, wall.at[part], wo_sem)
    w_load(1).start()
    for i in range(chunks):
        x_copy(i).start()
    w_load(2).start()
    w_load(0).start()
    wo_load.start()

    slots[...] = jnp.zeros_like(slots)
    slots[: pairs_ref.shape[0], : pairs_ref.shape[1]] = pairs_ref[...]
    listing[me] = slots[...]

    def own_rows(block):
        return pl.ds(pl.multiple_of(block * share, share), share)

    def hop1(step):
        peer = frame_peer(step)
        return pltpu.make_async_remote_copy(
            send1.at[peer], recv1.at[me], h1_send.at[step], h1_recv.at[step],
            device_id={"frames": peer}, device_id_type=MESH,
        )

    def hop2(step):
        peer = frame_peer(step)
        return pltpu.make_async_remote_copy(
            send2.at[peer], xs.at[me, own_rows(part)], h2_send.at[step], h2_recv.at[step],
            device_id={"frames": peer}, device_id_type=MESH,
        )

    def list_copy(step):
        return pltpu.make_async_remote_copy(
            slots, listing.at[me], list_send.at[step], list_recv.at[step],
            device_id={"frames": frame_peer(step)}, device_id_type=MESH,
        )

    pairwise = parts == 4
    near = part + 1 - 2 * lax.rem(part, 2)
    across = lax.rem(part + 2, parts)

    def w_copy(step):
        if pairwise:
            block = across if step == 2 else part
            peer = across if step == 0 else near
        else:
            block = part
            peer = head_peer(step)
        return pltpu.make_async_remote_copy(
            wall.at[block], wall.at[block], w_send.at[step], w_recv.at[step],
            device_id={"heads": peer}, device_id_type=MESH,
        )

    def slot_of(k):
        return lax.rem(me + devices - k, devices)

    def g_copy(k, step):
        block = part
        peer = head_peer(step)
        piece = xs.at[slot_of(k), own_rows(block)]
        return pltpu.make_async_remote_copy(
            piece, piece, g_send.at[k, step], g_recv.at[k, step],
            device_id={"heads": peer}, device_id_type=MESH,
        )

    def spread(k):
        for step in range(parts - 1):
            g_copy(k, step).start()

    def collect(k):
        for step in range(parts - 1):
            g_copy(k, step).wait()

    def m_copy(g, step):
        peer = head_peer(step)
        return pltpu.make_async_remote_copy(
            msend.at[g, peer], mrecv.at[g, part], m_send.at[g, step], m_recv.at[g, step],
            device_id={"heads": peer}, device_id_type=MESH,
        )

    def project(which, target, first):
        w_load(which).wait()

        def body(i, carry):
            if first:
                x_copy(i).wait()
            rows = x_ref[pl.ds(i * per, per)].reshape(per * length, width)
            made = jnp.dot(rows, w_ref[which], preferred_element_type=jnp.float32)
            target[pl.ds(i * per, per)] = made.astype(jnp.bfloat16).reshape(per, length, breadth)
            return carry

        lax.fori_loop(0, chunks, body, 0)

    project(1, k_ref, True)
    pl.semaphore_wait(barrier, devices + parts - 2)
    repeat(devices - 1, lambda s: list_copy(s).start())
    wo_load.wait()
    for s in range(2 if pairwise else parts - 1):
        w_copy(s).start()
    repeat(devices - 1, lambda s: list_copy(s).wait())
    to_scalar = pltpu.make_async_copy(listing, listing_s, local_sem)
    to_scalar.start()
    to_scalar.wait()

    def gather(owner):
        low = me * frames_here
        frame = jnp.int32(0)
        live = jnp.int32(-1)
        for entry in range(2 * cap):
            value = listing_s[owner, entry // 2, entry % 2]
            hit = (value >= low) & (value < low + frames_here)
            frame = jnp.where(hit, value - low, frame)
            live = jnp.where(hit, value - low, live)
        info[0, owner] = frame
        info[1, owner] = live
        send1[owner] = x_ref[frame, own_rows(part)]

    repeat(devices, gather)
    repeat(devices - 1, lambda s: hop1(s).start())
    recv1[me] = send1[me]

    project(2, v_ref, False)
    lane_head = lax.broadcasted_iota(jnp.int32, (length, breadth), 1) // HD

    def pick(array):
        shown = jnp.broadcast_to(array[:length], (length, breadth))
        for h in range(1, heads):
            shown = jnp.where(
                lane_head == h,
                jnp.broadcast_to(array[h * length : (h + 1) * length], (length, breadth)),
                shown,
            )
        return shown

    def lift(queries, key_rows):
        stacked = jnp.concatenate(
            [jnp.where(lane_head == h, queries, jnp.zeros_like(queries)) for h in range(heads)],
            axis=0,
        )
        scores = lax.dot_general(
            stacked, key_rows, (((1,), (1,)), ((), ())), preferred_element_type=jnp.float32
        ) * (HD ** -0.5)
        peak = jnp.max(scores, axis=1, keepdims=True)
        lifted = jnp.exp(scores - peak)
        total = jnp.sum(lifted, axis=1, keepdims=True)
        return lifted.astype(jnp.bfloat16), pick(peak), pick(total)

    def self_body(f, carry):
        e, m, l = lift(q_ref[f], k_ref[f])
        so[f] = pick(jnp.dot(e, v_ref[f], preferred_element_type=jnp.float32))
        sm[f] = m
        sl[f] = l
        return carry

    def relay(dest):
        low = dest * frames_here
        partner = me
        for row in range(cap):
            a = listing_s[me, row, 0]
            b = listing_s[me, row, 1]
            hit_a = (a >= low) & (a < low + frames_here)
            hit_b = (b >= low) & (b < low + frames_here)
            partner = jnp.where(hit_a, lax.div(b, jnp.int32(frames_here)), partner)
            partner = jnp.where(hit_b, lax.div(a, jnp.int32(frames_here)), partner)
        send2[dest] = recv1[partner]

    repeat(devices - 1, lambda s: hop1(s).wait())
    repeat(devices, relay)
    repeat(devices - 1, lambda s: hop2(s).start())
    xs[me, own_rows(part)] = send2[me]
    spread(0)
    project(0, q_ref, False)

    def pair_attend(k):
        owner = slot_of(k)
        rows = xs[owner]
        keys = jnp.dot(rows, w_ref[1], preferred_element_type=jnp.float32).astype(jnp.bfloat16)
        values = jnp.dot(rows, w_ref[2], preferred_element_type=jnp.float32).astype(jnp.bfloat16)
        e, m, l = lift(q_ref[info[0, owner]], keys)
        po[owner] = pick(jnp.dot(e, values, preferred_element_type=jnp.float32))
        pm[owner] = m
        psum[owner] = l

    def arrived(step):
        hop2(step).wait()
        spread(step + 1)

    def finish(k):
        collect(k)
        pair_attend(k)

    repeat(devices - 1, arrived)
    lax.fori_loop(0, frames_here, self_body, 0)

    if pairwise:
        w_copy(0).wait()
        w_copy(2).start()
    finish(0)
    repeat(devices - 1, lambda s: finish(s + 1))


    def peak_body(f, carry):
        def raise_peak(owner, peak):
            return jnp.maximum(peak, jnp.where(info[1, owner] == f, pm[owner], -jnp.inf))

        peak = lax.fori_loop(0, devices, raise_peak, sm[f], unroll=devices <= 8)
        top[f] = peak
        weight = jnp.exp(sm[f] - peak)
        sm[f] = weight
        sl[f] = weight * sl[f]
        return carry

    lax.fori_loop(0, frames_here, peak_body, 0)

    def pair_weight(owner):
        live = info[1, owner] >= 0
        weight = jnp.where(live, jnp.exp(pm[owner] - top[info[0, owner]]), 0.0)
        weight = jnp.where(live, weight, 0.0)
        pm[owner] = weight
        psum[owner] = weight * psum[owner]

    repeat(devices, pair_weight)

    def den_body(f, carry):
        def add(owner, den):
            return den + jnp.where(info[1, owner] == f, psum[owner], 0.0)

        den = lax.fori_loop(0, devices, add, sl[f], unroll=devices <= 8)
        inverse = 1.0 / den
        top[f] = inverse
        so[f] = so[f] * (sm[f] * inverse)
        return carry

    lax.fori_loop(0, frames_here, den_body, 0)

    def pair_scale(owner):
        po[owner] = po[owner] * (pm[owner] * top[info[0, owner]])

    repeat(devices, pair_scale)

    for g in range(groups_out):

        def merge_body(i, carry):
            f = g * group + i

            def add(owner, state):
                return state + jnp.where(info[1, owner] == f, po[owner], 0.0)

            merged = lax.fori_loop(0, devices, add, so[f], unroll=devices <= 8)
            merged = merged.astype(jnp.bfloat16)
            for h in range(parts):
                msend[g, h, i] = merged[h * share : (h + 1) * share]
            return carry

        lax.fori_loop(0, group, merge_body, 0)
        for s in range(parts - 1):
            m_copy(g, s).start()
        mrecv[g, part] = msend[g, part]

    for s in range(1 if pairwise else 0, parts - 1):
        w_copy(s).wait()
    for g in range(groups_out):
        for s in range(parts - 1):
            m_copy(g, s).wait()
        total = jnp.zeros((group * share, width), jnp.float32)
        for h in range(parts):
            total = total + jnp.dot(
                mrecv[g, h].reshape(group * share, breadth),
                wall[h],
                preferred_element_type=jnp.float32,
            )
        out_ref[pl.ds(g * group, group)] = total.astype(jnp.bfloat16).reshape(
            group, share, width
        )


def local(tokens, w_qkv, w_out, pair_slots):
    frames_here, length, width = tokens.shape
    breadth = w_qkv.shape[2]
    devices = lax.axis_size("frames")
    parts = lax.axis_size("heads")
    cap = pair_slots.shape[0]
    share = length // parts
    rows = -(-cap // 8) * 8
    groups_out = 2
    group = frames_here // groups_out
    bf, f32 = jnp.bfloat16, jnp.float32
    vm = pl.BlockSpec(memory_space=pltpu.VMEM)
    hbm = pl.BlockSpec(memory_space=pl.ANY)
    dma = pltpu.SemaphoreType.DMA
    frame_bf = pltpu.VMEM((frames_here, length, breadth), bf)
    frame_f = pltpu.VMEM((frames_here, length, breadth), f32)
    slot_bf = pltpu.VMEM((devices, share, width), bf)
    slot_f = pltpu.VMEM((devices, length, breadth), f32)
    return pl.pallas_call(
        functools.partial(kernel, devices, parts, cap, groups_out),
        out_shape=jax.ShapeDtypeStruct((frames_here, share, width), bf),
        in_specs=[vm, hbm, hbm, hbm],
        out_specs=vm,
        scratch_shapes=[
            pltpu.VMEM((frames_here, length, width), bf),
            pltpu.VMEM((3, width, breadth), bf),
            pltpu.VMEM((rows, 128), jnp.int32),
            pltpu.VMEM((devices, rows, 128), jnp.int32),
            pltpu.SMEM((devices, rows, 128), jnp.int32),
            pltpu.SMEM((2, devices), jnp.int32),
        ]
        + [frame_bf] * 3
        + [slot_bf] * 3
        + [pltpu.VMEM((devices, length, width), bf)]
        + [frame_f] * 4
        + [slot_f] * 3
        + [
            pltpu.VMEM((groups_out, parts, group, share, breadth), bf),
            pltpu.VMEM((groups_out, parts, group, share, breadth), bf),
            pltpu.VMEM((parts, breadth, width), bf),
            dma((frames_here * length // 256,)),
            dma((3,)),
            dma,
            dma((devices - 1,)),
            dma((devices - 1,)),
            dma,
        ]
        + [dma((devices - 1,))] * 4
        + [dma((devices, parts - 1))] * 2
        + [dma((parts - 1,))] * 2
        + [dma((groups_out, parts - 1))] * 2,
        compiler_params=pltpu.CompilerParams(
            collective_id=0, has_side_effects=True, vmem_limit_bytes=60 * 1024 * 1024
        ),
    )(
        pair_slots,
        tokens,
        jnp.transpose(w_qkv, (1, 0, 2)),
        w_out,
    )


def solution(mesh):
    placed = (
        P(("groups", "frames"), None, None),
        P(None, None, "heads"),
        P("heads", None),
        P(("groups", "frames"), None),
    )
    return jax.shard_map(
        local,
        mesh=mesh,
        in_specs=placed,
        out_specs=P(("groups", "frames"), "heads", None),
        check_vma=False,
    )
```
